32 devices in a mesh: row: 4 (over x, core), col: 8 (over z, y).
Axes of the slice: x: 2, y: 2, z: 4, core: 2. Of those that a mesh axis runs over, the one named last changes fastest.
Arguments:
- kernel: bfloat16 [32768, 32768], P('row', 'col'), may hold values from -1 to 1
- random_cols: bfloat16 [32768, 256], P('row'), may hold values from -6 to 6
- tree_perm: int32 [32768], replicated, may hold values from 0 to 32767, as said below
- leaf_units: int32 [32], replicated, may hold values from 1 to 8, 160 in all
Outputs:
- bases: bfloat16 [4, 32768, 256], P(None, ('row', 'col'))
The draws below stay inside these ranges and needn't reach their ends.
Inputs may be any that keep to these rules, and one draw needn't show every extreme that they name: `tree_perm`: A permutation. Cut tree positions and stored rows alike into blocks of 1024 in order: every tree block takes at most 32 rows from any one stored block, some pair of blocks shares exactly 32, and every stored block gives 1024 rows in all. `leaf_units`: they sum to 160.
All inputs are finite; a program needn't handle non-finite values.
Results may differ from the reference program's by a relative error of at most 0.0067.
Values may be sent and summed in bfloat16 or wider, within the bound.
A program may use at most 192 MiB of HBM per device.

```python
import math
import jax
import jax.numpy as jnp
import numpy as np
from jax import lax

N = 32768
S = 256
UNIT = 128
MINU = 4
MOSTU = 8
LEAVES = 32
LEVELS = 3
ROWS_DEV = 1024


def draw_kernel(key, part):
    point_key, noise_key, weight_key = jax.random.split(key, 3)
    spread_width = 0.08
    amplitude = 0.5
    points = jax.random.uniform(point_key, (N, 3), jnp.float32)
    norms = jnp.sum(points * points, axis=1)
    block = min(N, 512)
    groups = N // ROWS_DEV
    spacing = jax.random.permutation(weight_key, groups).astype(jnp.float32) / max(groups - 1, 1)
    group_weight = jnp.exp(jnp.log(10.0) * spacing)
    row_weight = jnp.repeat(group_weight, ROWS_DEV, total_repeat_length=N)

    def one_block(index):
        chosen = lax.dynamic_slice_in_dim(points, index * block, block, 0)
        chosen_norms = lax.dynamic_slice_in_dim(norms, index * block, block, 0)
        chosen_weight = lax.dynamic_slice_in_dim(row_weight, index * block, block, 0)
        cross = jnp.dot(chosen, points.T, precision=lax.Precision.HIGHEST)
        distance = jnp.maximum(chosen_norms[:, None] + norms[None, :] - 2.0 * cross, 0.0)
        noise = jax.random.truncated_normal(jax.random.fold_in(noise_key, index), -4.0, 4.0, (block, N), jnp.float32)
        entries = (jnp.exp(-distance / (2.0 * spread_width * spread_width)) + amplitude * noise) * N ** (-0.5)
        return (entries * chosen_weight[:, None]).astype(jnp.bfloat16)
    blocks = lax.map(one_block, jnp.arange(N // block, dtype=jnp.int32))
    return blocks.reshape(N, N)


def random_rows(key, count, length):
    scores = jax.random.randint(key, (count, length), 0, 2 ** 20) * length + jnp.arange(length, dtype=jnp.int32)[None, :]
    return jnp.argsort(scores, axis=1).astype(jnp.int32)


def draw_tree_perm(key, part):
    devices = N // ROWS_DEV
    first_key, second_key, third_key = jax.random.split(jax.random.fold_in(key, 17), 3)
    device_order = jax.random.permutation(first_key, devices).astype(jnp.int32)
    within = random_rows(second_key, devices, ROWS_DEV)
    base = (jnp.arange(devices, dtype=jnp.int32) * ROWS_DEV)[:, None]
    source = jnp.take(device_order, (within + base) % devices).reshape(-1)
    grouped = jnp.argsort(source * N + jnp.arange(N, dtype=jnp.int32)).astype(jnp.int32)
    ranks = random_rows(third_key, devices, ROWS_DEV)
    stored = (base + ranks).reshape(-1)
    return jnp.zeros((N,), jnp.int32).at[grouped].set(stored)


def levels(stream_key, dims, cuts, smallest, largest):
    level = 1.0
    for position, blocks in cuts:
        steps = jax.random.uniform(jax.random.fold_in(jax.random.fold_in(stream_key, 6), position), (blocks,), jnp.float32, smallest / len(cuts), largest / len(cuts))
        level = level * jnp.repeat(jnp.exp(steps), dims[position] // blocks).reshape((-1,) + (1,) * (len(dims) - 1 - position))
    return level


def profile(count, total, bound, lean):
    loads = [(1 << 20) // math.isqrt(standing ** lean) + 1 for standing in range(2, count + 1)]
    surplus, counts = total - bound - (count - 1), [1] * (count - 1)
    while surplus > 0:
        candidates = [i for i in range(count - 1) if counts[i] < bound]
        whole, left = sum([loads[i] for i in candidates]), surplus
        for i in candidates:
            extra = min(bound - counts[i], max(1, left * loads[i] // whole), surplus)
            counts[i] = counts[i] + extra
            surplus = surplus - extra
    return np.array([bound] + counts)


def uneven(rng, number_of, total, most, skew):
    if number_of == 2:
        one = jax.random.randint(rng, (), max(1, total - most), min(most, total - 1) + 1)
        return jnp.stack([one, total - one])
    lengths = jnp.asarray(profile(number_of, total, most, skew), jnp.int32)
    twos = (number_of - 1) // 2
    giver, taker = lengths[1:1 + 2 * twos:2], lengths[2:2 + 2 * twos:2]
    room = jnp.minimum(giver - 1, most - taker)
    moved = jax.random.randint(jax.random.fold_in(rng, 1), (twos,), 0, 1 << 20) % (room + 1)
    lengths = lengths.at[1:1 + 2 * twos:2].set(giver - moved).at[2:2 + 2 * twos:2].set(taker + moved)
    return lengths[jax.random.permutation(jax.random.fold_in(rng, 2), number_of)]


def centred(rng, shape, deviation, reach, cuts=(), kind=jnp.bfloat16):
    factor_of = levels(rng, shape, cuts, -0.22, 0.18) if cuts else 1.0
    drawn = jax.random.normal(rng, shape, jnp.float32) * deviation * factor_of
    return jnp.minimum(jnp.maximum(drawn, -reach), reach).astype(kind)


def setup_inputs(seed: int = 0) -> dict:
    key_list = jax.random.split(jax.random.key(seed), 5)
    return {
        "kernel": draw_kernel(jax.random.fold_in(key_list[4], 71), 0),
        "random_cols": centred(key_list[1], (N, S), 1.0, 6.0, ((0, 4),)),
        "tree_perm": draw_tree_perm(jax.random.fold_in(key_list[4], 71), 0),
        "leaf_units": uneven(key_list[3], LEAVES, N // UNIT - (MINU - 1) * LEAVES, MOSTU, 1).astype(jnp.int32),
    }


def reference(kernel, random_cols, tree_perm, leaf_units):
    partial_w = lax.dot_general(kernel.astype(jnp.float32), random_cols.astype(jnp.float32), (((0,), (0,)), ((), ())), preferred_element_type=jnp.float32)
    sample_w = partial_w.astype(jnp.bfloat16)
    sample = jnp.dot(kernel.astype(jnp.float32), sample_w.astype(jnp.float32), preferred_element_type=jnp.float32).astype(jnp.bfloat16)
    tree_rows = jnp.take(sample, tree_perm.astype(jnp.int32), axis=0)
    sizes = (UNIT * (MINU - 1 + leaf_units)).astype(jnp.int32)
    ends = jnp.cumsum(sizes).astype(jnp.int32)
    positions = jnp.arange(N, dtype=jnp.int32)
    leaf_of = jnp.sum(positions[:, None] >= ends[None, :], axis=1).astype(jnp.int32)

    def leaf_gram(leaf):
        masked = jnp.where((leaf_of == leaf)[:, None], tree_rows, jnp.zeros((), jnp.bfloat16))
        return jnp.dot(masked.T.astype(jnp.float32), tree_rows.astype(jnp.float32), preferred_element_type=jnp.float32)
    leaf_grams = lax.map(leaf_gram, jnp.arange(LEAVES, dtype=jnp.int32))
    values = tree_rows.astype(jnp.float32)
    results = []
    for level in range(LEVELS + 1):
        group = 2 ** level
        count = LEAVES // group
        node_grams = leaf_grams.reshape(count, group, S, S).sum(axis=1)
        node_sizes = sizes.reshape(count, group).sum(axis=1).astype(jnp.float32)
        factor = jnp.linalg.cholesky(node_grams / node_sizes[:, None, None])
        node_of = leaf_of // group

        def add_node(total, node):
            solved = jax.scipy.linalg.solve_triangular(factor[node], values.T, lower=True).T
            return (total + jnp.where((node_of == node)[:, None], solved, jnp.zeros((), jnp.float32)), None)
        total, unused = lax.scan(add_node, jnp.zeros((N, S), jnp.float32), jnp.arange(count, dtype=jnp.int32))
        results.append(total.astype(jnp.bfloat16))
    return jnp.stack(results)
```

```python
import functools

import jax
import jax.numpy as jnp
from jax import lax
from jax.experimental import pallas as pl
from jax.experimental.pallas import tpu as pltpu
from jax.sharding import PartitionSpec as P

UNIT = 128
MINU = 4
MOSTU = 8
LEVELS = 3
BLOCK = 64
HIGHEST = lax.Precision.HIGHEST


def basis_kernel(index_ref, gram_ref, rows_ref, out_ref, work, block, high, low):
    nodes, width, _ = gram_ref.shape
    count = width // BLOCK
    eye = (
        lax.broadcasted_iota(jnp.int32, (width, width), 0)
        == lax.broadcasted_iota(jnp.int32, (width, width), 1)
    ).astype(jnp.float32)

    @pl.loop(0, nodes)
    def _(node):
        work[node, :, :width] = gram_ref[node]
        work[node, :, width:] = eye

    small = (
        lax.broadcasted_iota(jnp.int32, (nodes, BLOCK, BLOCK), 1)
        == lax.broadcasted_iota(jnp.int32, (nodes, BLOCK, BLOCK), 2)
    )

    @pl.loop(0, count)
    def _(step):
        for which in range(count):

            @pl.when(step == which)
            def _():
                start = which * BLOCK
                block[:, :, :BLOCK] = work[:, start : start + BLOCK, start : start + BLOCK]
                block[:, :, BLOCK:] = small.astype(jnp.float32)

        for column in range(BLOCK - 1):
            base = column // 8 * 8
            rest = block[:, base:, :]
            pivot_row = rest[:, column - base : column - base + 1, :]
            scale = 1.0 / pivot_row[:, :, column : column + 1]
            below = (
                lax.broadcasted_iota(jnp.int32, (nodes, BLOCK - base, 1), 1) > column - base
            )
            factor = jnp.where(below, rest[:, :, column : column + 1], 0.0)
            block[:, base:, :] = rest - factor * (pivot_row * scale)
        pivots = jnp.sum(jnp.where(small, block[:, :, :BLOCK], 0.0), axis=2, keepdims=True)
        block[:, :, BLOCK:] = block[:, :, BLOCK:] * lax.rsqrt(pivots)

        for which in range(count):

            @pl.when(step == which)
            def _():
                start = which * BLOCK
                after = start + BLOCK
                left = start // 128 * 128
                right = width + (after + 127) // 128 * 128

                @pl.loop(0, nodes)
                def _(node):
                    inverse = block[node][:, BLOCK:]
                    solved = jnp.dot(
                        inverse,
                        work[node, start:after, left:right],
                        preferred_element_type=jnp.float32,
                        precision=HIGHEST,
                    )
                    work[node, start:after, left:right] = solved
                    if after < width:
                        panel = solved[:, : width - left].T
                        change = jnp.dot(
                            panel[after - left :, :],
                            solved,
                            preferred_element_type=jnp.float32,
                            precision=HIGHEST,
                        )
                        work[node, after:, left:right] = work[node, after:, left:right] - change

    @pl.loop(0, nodes)
    def _(node):
        full = work[node, :, width:]
        top = full.astype(jnp.bfloat16)
        high[node] = top
        low[node] = (full - top.astype(jnp.float32)).astype(jnp.bfloat16)

    levels, rows, _ = out_ref.shape
    units = rows // UNIT

    @pl.loop(0, levels)
    def _(level):
        @pl.loop(0, units)
        def _(unit):
            node = index_ref[level * units + unit]
            where = pl.ds(pl.multiple_of(unit * UNIT, UNIT), UNIT)
            values = rows_ref[where, :]
            contract = (((1,), (1,)), ((), ()))
            total = lax.dot_general(
                values, low[node], contract, preferred_element_type=jnp.float32
            ) + lax.dot_general(values, high[node], contract, preferred_element_type=jnp.float32)
            out_ref[level, where, :] = total.astype(jnp.bfloat16)


def make_bases(index, grams, rows, levels):
    nodes, width, _ = grams.shape
    return pl.pallas_call(
        basis_kernel,
        out_shape=jax.ShapeDtypeStruct((levels, rows.shape[0], width), jnp.bfloat16),
        in_specs=[
            pl.BlockSpec(memory_space=pltpu.SMEM),
            pl.BlockSpec(memory_space=pltpu.VMEM),
            pl.BlockSpec(memory_space=pltpu.VMEM),
        ],
        out_specs=pl.BlockSpec(memory_space=pltpu.VMEM),
        scratch_shapes=[
            pltpu.VMEM((nodes, width, 2 * width), jnp.float32),
            pltpu.VMEM((nodes, BLOCK, 2 * BLOCK), jnp.float32),
            pltpu.VMEM((nodes, width, width), jnp.bfloat16),
            pltpu.VMEM((nodes, width, width), jnp.bfloat16),
        ],
        compiler_params=pltpu.CompilerParams(vmem_limit_bytes=40 * 2**20),
    )(index, grams, rows)


def to_tree_order(sample, tree_perm):
    rows_dev, width = sample.shape
    devices = tree_perm.shape[0] // rows_dev
    device = lax.axis_index(("row", "col"))
    capacity = (rows_dev + devices - 1) // devices
    grid = tree_perm.reshape(devices, rows_dev)
    mine = grid // rows_dev == device
    rank = jnp.cumsum(mine.astype(jnp.int32), axis=1) - 1
    slots = jnp.arange(capacity, dtype=jnp.int32)
    chosen = mine[:, None, :] & (rank[:, None, :] == slots[None, :, None])
    send = jnp.sum(jnp.where(chosen, (grid % rows_dev)[:, None, :], 0), axis=2).reshape(-1)
    outgoing = jnp.take(sample, send, axis=0, mode="clip")
    incoming = lax.all_to_all(outgoing, ("row", "col"), split_axis=0, concat_axis=0, tiled=True)
    wanted = lax.dynamic_slice_in_dim(tree_perm, device * rows_dev, rows_dev)
    source = wanted // rows_dev
    order = jnp.arange(rows_dev, dtype=jnp.int32)
    ahead = (source[None, :] == source[:, None]) & (order[None, :] < order[:, None])
    pick = source * capacity + jnp.sum(ahead, axis=1)
    return jnp.take(incoming, pick, axis=0, mode="clip")


def bases_of(sample, tree_perm, leaf_units):
    rows_dev, width = sample.shape
    devices = tree_perm.shape[0] // rows_dev
    device = lax.axis_index(("row", "col"))
    tree_rows = to_tree_order(sample, tree_perm)
    sizes = UNIT * (MINU - 1 + leaf_units)
    leaves = sizes.shape[0]
    ends = jnp.cumsum(sizes)
    levels = LEVELS + 1
    units = rows_dev // UNIT
    starts = jnp.arange(devices, dtype=jnp.int32) * rows_dev
    first_leaf = jnp.sum(starts[:, None] >= ends[None, :], axis=1)
    last_leaf = jnp.sum((starts + rows_dev - 1)[:, None] >= ends[None, :], axis=1)
    unit_start = device * rows_dev + jnp.arange(units, dtype=jnp.int32) * UNIT
    unit_leaf = jnp.sum(unit_start[:, None] >= ends[None, :], axis=1)

    reach = [2 + max(rows_dev - 2 * UNIT, 0) // (UNIT * MINU * 2**t) for t in range(levels)]
    first = jnp.take(first_leaf, device)
    touched = first + jnp.arange(reach[0], dtype=jnp.int32)
    unit_mask = (unit_leaf[None, :] == touched[:, None]).astype(jnp.bfloat16)
    mask = jnp.repeat(unit_mask, UNIT, axis=1)
    partial = jnp.stack(
        [
            lax.dot_general(
                tree_rows * mask[which][:, None],
                tree_rows,
                (((0,), (0,)), ((), ())),
                preferred_element_type=jnp.float32,
            )
            for which in range(reach[0])
        ]
    )

    def pick_nodes(level, nodes):
        chosen = touched // 2**level == nodes
        return jnp.sum(jnp.where(chosen[:, None, None], partial, 0.0), axis=0)

    wanted = []
    local = LEVELS - 1
    for level in range(local):
        group = 2**level
        low, high = first_leaf // group, last_leaf // group
        my_low, my_high = jnp.take(low, device), jnp.take(high, device)
        span = (UNIT * (MINU - 1 + MOSTU) * group - 2 * UNIT) // rows_dev + 1
        head, tail = pick_nodes(level, my_low), pick_nodes(level, my_high)
        to_head = jnp.zeros_like(head)
        to_tail = jnp.zeros_like(head)
        for shift in range(1, span + 1):
            up = lax.ppermute(
                tail, ("row", "col"), [(i, i + shift) for i in range(devices - shift)]
            )
            down = lax.ppermute(
                head, ("row", "col"), [(i + shift, i) for i in range(devices - shift)]
            )
            before = jnp.take(high, jnp.maximum(device - shift, 0))
            behind = jnp.take(low, jnp.minimum(device + shift, devices - 1))
            use_up = (device >= shift) & (before == my_low)
            use_down = (device + shift < devices) & (behind == my_high)
            to_head = to_head + jnp.where(use_up, up, 0.0)
            to_tail = to_tail + jnp.where(use_down, down, 0.0)
        for which in range(reach[level]):
            node = my_low + which
            gram = pick_nodes(level, node)
            gram = gram + jnp.where(node == my_low, to_head, 0.0)
            wanted.append(gram + jnp.where(node == my_high, to_tail, 0.0))
    group = 2**local
    count = leaves // group
    spread = jnp.stack([pick_nodes(local, node) for node in range(count)])
    shared = lax.psum(spread, ("row", "col"))
    for level in range(local, levels):
        grams = shared.reshape(leaves // 2**level, 2 ** (level - local), width, width).sum(axis=1)
        index = first // 2**level + jnp.arange(reach[level], dtype=jnp.int32)
        taken = jnp.take(grams, jnp.minimum(index, leaves // 2**level - 1), axis=0)
        wanted.extend(taken[which] for which in range(reach[level]))

    slot = 0
    last = jnp.take(last_leaf, device)
    eye = jnp.eye(width, dtype=jnp.float32)
    index = []
    for level in range(levels):
        group = 2**level
        node_sizes = sizes.reshape(leaves // group, group).sum(axis=1)
        low, high = first // group, last // group
        for which in range(reach[level]):
            node = low + which
            rows = jnp.take(node_sizes, jnp.minimum(node, leaves // group - 1))
            mean = wanted[slot + which] / rows.astype(jnp.float32)
            wanted[slot + which] = jnp.where(node <= high, mean, eye)
        index.append(slot + unit_leaf // group - low)
        slot += reach[level]
    return make_bases(jnp.concatenate(index), jnp.stack(wanted), tree_rows, levels)


def shards(kernel, random_cols, tree_perm, leaf_units):
    width = random_cols.shape[1]
    parts = lax.axis_size("row")
    partial_w = lax.dot_general(
        kernel, random_cols, (((0,), (0,)), ((), ())), preferred_element_type=jnp.float32
    ).astype(jnp.bfloat16)
    pieces = lax.all_to_all(partial_w, "row", split_axis=0, concat_axis=0, tiled=True)
    piece = jnp.sum(pieces.reshape(parts, -1, width).astype(jnp.float32), axis=0)
    sample_w = lax.all_gather(piece.astype(jnp.bfloat16), "row", axis=0, tiled=True)
    columns = lax.axis_size("col")
    partial = jnp.dot(kernel, sample_w, preferred_element_type=jnp.float32).astype(jnp.bfloat16)
    pieces = lax.all_to_all(partial, "col", split_axis=0, concat_axis=0, tiled=True)
    sample = jnp.sum(pieces.reshape(columns, -1, width).astype(jnp.float32), axis=0)
    return bases_of(sample.astype(jnp.bfloat16), tree_perm, leaf_units)


def solution(mesh):
    return jax.shard_map(
        shards,
        mesh=mesh,
        in_specs=(P("row", "col"), P("row", None), P(), P()),
        out_specs=P(None, ("row", "col"), None),
        check_vma=False,
    )
```

```python
import jax
import jax.numpy as jnp
from jax import lax
from jax.experimental import pallas as pl
from jax.experimental.pallas import tpu as pltpu
from jax.sharding import PartitionSpec as P

UNIT = 128
MINU = 4
MOSTU = 8
LEVELS = 3
BLOCK = 64
HIGHEST = lax.Precision.HIGHEST


def basis_kernel(index_ref, gram_ref, rows_ref, out_ref, work, block, high, low):
    nodes, width, _ = gram_ref.shape
    count = width // BLOCK
    eye = (
        lax.broadcasted_iota(jnp.int32, (width, width), 0)
        == lax.broadcasted_iota(jnp.int32, (width, width), 1)
    ).astype(jnp.float32)

    @pl.loop(0, nodes)
    def _(node):
        work[node, :, :width] = gram_ref[node]
        work[node, :, width:] = eye

    small = (
        lax.broadcasted_iota(jnp.int32, (nodes, BLOCK, BLOCK), 1)
        == lax.broadcasted_iota(jnp.int32, (nodes, BLOCK, BLOCK), 2)
    )

    @pl.loop(0, count)
    def _(step):
        for which in range(count):

            @pl.when(step == which)
            def _():
                start = which * BLOCK
                block[:, :, :BLOCK] = work[:, start : start + BLOCK, start : start + BLOCK]
                block[:, :, BLOCK:] = small.astype(jnp.float32)

        for column in range(BLOCK - 1):
            base = column // 8 * 8
            rest = block[:, base:, :]
            pivot_row = rest[:, column - base : column - base + 1, :]
            scale = 1.0 / pivot_row[:, :, column : column + 1]
            below = (
                lax.broadcasted_iota(jnp.int32, (nodes, BLOCK - base, 1), 1) > column - base
            )
            factor = jnp.where(below, rest[:, :, column : column + 1], 0.0)
            block[:, base:, :] = rest - factor * (pivot_row * scale)
        pivots = jnp.sum(jnp.where(small, block[:, :, :BLOCK], 0.0), axis=2, keepdims=True)
        block[:, :, BLOCK:] = block[:, :, BLOCK:] * lax.rsqrt(pivots)

        for which in range(count):

            @pl.when(step == which)
            def _():
                start = which * BLOCK
                after = start + BLOCK
                left = start // 128 * 128
                right = width + (after + 127) // 128 * 128

                @pl.loop(0, nodes)
                def _(node):
                    inverse = block[node][:, BLOCK:]
                    solved = jnp.dot(
                        inverse,
                        work[node, start:after, left:right],
                        preferred_element_type=jnp.float32,
                        precision=HIGHEST,
                    )
                    work[node, start:after, left:right] = solved
                    if after < width:
                        panel = solved[:, : width - left].T
                        change = jnp.dot(
                            panel[after - left :, :],
                            solved,
                            preferred_element_type=jnp.float32,
                            precision=HIGHEST,
                        )
                        work[node, after:, left:right] = work[node, after:, left:right] - change

    @pl.loop(0, nodes)
    def _(node):
        full = work[node, :, width:]
        top = full.astype(jnp.bfloat16)
        high[node] = top
        low[node] = (full - top.astype(jnp.float32)).astype(jnp.bfloat16)

    levels, rows, _ = out_ref.shape
    units = rows // UNIT

    @pl.loop(0, levels)
    def _(level):
        @pl.loop(0, units)
        def _(unit):
            node = index_ref[level * units + unit]
            where = pl.ds(pl.multiple_of(unit * UNIT, UNIT), UNIT)
            values = rows_ref[where, :]
            contract = (((1,), (1,)), ((), ()))
            total = lax.dot_general(
                values, low[node], contract, preferred_element_type=jnp.float32
            ) + lax.dot_general(values, high[node], contract, preferred_element_type=jnp.float32)
            out_ref[level, where, :] = total.astype(jnp.bfloat16)


def make_bases(index, grams, rows, levels):
    nodes, width, _ = grams.shape
    return pl.pallas_call(
        basis_kernel,
        out_shape=jax.ShapeDtypeStruct((levels, rows.shape[0], width), jnp.bfloat16),
        in_specs=[
            pl.BlockSpec(memory_space=pltpu.SMEM),
            pl.BlockSpec(memory_space=pltpu.VMEM),
            pl.BlockSpec(memory_space=pltpu.VMEM),
        ],
        out_specs=pl.BlockSpec(memory_space=pltpu.VMEM),
        scratch_shapes=[
            pltpu.VMEM((nodes, width, 2 * width), jnp.float32),
            pltpu.VMEM((nodes, BLOCK, 2 * BLOCK), jnp.float32),
            pltpu.VMEM((nodes, width, width), jnp.bfloat16),
            pltpu.VMEM((nodes, width, width), jnp.bfloat16),
        ],
        compiler_params=pltpu.CompilerParams(vmem_limit_bytes=40 * 2**20),
    )(index, grams, rows)


def to_tree_order(sample, tree_perm):
    rows_dev, width = sample.shape
    devices = tree_perm.shape[0] // rows_dev
    device = lax.axis_index(("row", "col"))
    capacity = (rows_dev + devices - 1) // devices
    grid = tree_perm.reshape(devices, rows_dev)
    mine = grid // rows_dev == device
    rank = jnp.cumsum(mine.astype(jnp.int32), axis=1) - 1
    slots = jnp.arange(capacity, dtype=jnp.int32)
    chosen = mine[:, None, :] & (rank[:, None, :] == slots[None, :, None])
    send = jnp.sum(jnp.where(chosen, (grid % rows_dev)[:, None, :], 0), axis=2).reshape(-1)
    outgoing = jnp.take(sample, send, axis=0, mode="clip")
    incoming = lax.all_to_all(outgoing, ("row", "col"), split_axis=0, concat_axis=0, tiled=True)
    wanted = lax.dynamic_slice_in_dim(tree_perm, device * rows_dev, rows_dev)
    source = wanted // rows_dev
    order = jnp.arange(rows_dev, dtype=jnp.int32)
    ahead = (source[None, :] == source[:, None]) & (order[None, :] < order[:, None])
    pick = source * capacity + jnp.sum(ahead, axis=1)
    return jnp.take(incoming, pick, axis=0, mode="clip")


def bases_of(sample, tree_perm, leaf_units):
    rows_dev, width = sample.shape
    devices = tree_perm.shape[0] // rows_dev
    device = lax.axis_index(("row", "col"))
    tree_rows = to_tree_order(sample, tree_perm)
    sizes = UNIT * (MINU - 1 + leaf_units)
    leaves = sizes.shape[0]
    ends = jnp.cumsum(sizes)
    levels = LEVELS + 1
    units = rows_dev // UNIT
    starts = jnp.arange(devices, dtype=jnp.int32) * rows_dev
    first_leaf = jnp.sum(starts[:, None] >= ends[None, :], axis=1)
    last_leaf = jnp.sum((starts + rows_dev - 1)[:, None] >= ends[None, :], axis=1)
    unit_start = device * rows_dev + jnp.arange(units, dtype=jnp.int32) * UNIT
    unit_leaf = jnp.sum(unit_start[:, None] >= ends[None, :], axis=1)

    reach = [2 + max(rows_dev - 2 * UNIT, 0) // (UNIT * MINU * 2**t) for t in range(levels)]
    half = width // 2
    first = jnp.take(first_leaf, device)
    touched = first + jnp.arange(reach[0], dtype=jnp.int32)
    unit_mask = (unit_leaf[None, :] == touched[:, None]).astype(jnp.bfloat16)
    mask = jnp.repeat(unit_mask, UNIT, axis=1)
    packed = []
    for which in range(reach[0]):
        full = lax.dot_general(
            tree_rows * mask[which][:, None],
            tree_rows,
            (((0,), (0,)), ((), ())),
            preferred_element_type=jnp.float32,
        )
        packed.append(jnp.concatenate([full[:, :half], full[half:, half:]], axis=0))
    partial = jnp.stack(packed)

    def pick_nodes(level, nodes):
        chosen = touched // 2**level == nodes
        return jnp.sum(jnp.where(chosen[:, None, None], partial, 0.0), axis=0)

    lows = jnp.stack([first_leaf // 2**level for level in range(levels)])
    highs = jnp.stack([last_leaf // 2**level for level in range(levels)])
    my_low = jnp.take(lows, device, axis=1)
    my_high = jnp.take(highs, device, axis=1)
    spans = [
        (UNIT * (MINU - 1 + MOSTU) * 2**level - 2 * UNIT) // rows_dev + 1 for level in range(levels)
    ]

    def gathered(sign, edge, theirs, shared, mine):
        def moved(value, shift, ids, start):
            pairs = [(i, i + shift) for i in range(devices - shift)]
            if sign < 0:
                pairs = [(j, i) for i, j in pairs]
            got = lax.ppermute(value, ("row", "col"), pairs)
            other = device - sign * shift
            inside = (other >= 0) & (other < devices)
            named = jnp.take(ids, jnp.clip(other, 0, devices - 1), axis=1)
            keep = inside & (named == mine)[start:]
            return jnp.where(keep[:, None, None], got, 0.0)

        total = moved(edge, 1, theirs, 0)
        covered = 1
        while covered < min(max(spans), devices - 1):
            start = sum(span <= covered for span in spans)
            more = total[start:] + moved(total[start:], covered, shared, start)
            total = jnp.concatenate([total[:start], more]) if start else more
            covered *= 2
        return total

    tails = jnp.stack([pick_nodes(level, my_high[level]) for level in range(levels)])
    heads = jnp.stack([pick_nodes(level, my_low[level]) for level in range(levels)])
    to_head = gathered(1, tails, highs, lows, my_low)
    to_tail = gathered(-1, heads, lows, highs, my_high)
    wanted = []
    for level in range(levels):
        for which in range(reach[level]):
            node = my_low[level] + which
            gram = pick_nodes(level, node)
            gram = gram + jnp.where(node == my_low[level], to_head[level], 0.0)
            gram = gram + jnp.where(node == my_high[level], to_tail[level], 0.0)
            top = jnp.concatenate([gram[:half], gram[half:width].T], axis=1)
            bottom = jnp.concatenate([gram[half:width], gram[width:]], axis=1)
            wanted.append(jnp.concatenate([top, bottom], axis=0))

    slot = 0
    last = jnp.take(last_leaf, device)
    eye = jnp.eye(width, dtype=jnp.float32)
    index = []
    for level in range(levels):
        group = 2**level
        node_sizes = sizes.reshape(leaves // group, group).sum(axis=1)
        low, high = first // group, last // group
        for which in range(reach[level]):
            node = low + which
            rows = jnp.take(node_sizes, jnp.minimum(node, leaves // group - 1))
            mean = wanted[slot + which] / rows.astype(jnp.float32)
            wanted[slot + which] = jnp.where(node <= high, mean, eye)
        index.append(slot + unit_leaf // group - low)
        slot += reach[level]
    return make_bases(jnp.concatenate(index), jnp.stack(wanted), tree_rows, levels)


def shards(kernel, random_cols, tree_perm, leaf_units):
    width = random_cols.shape[1]
    parts = lax.axis_size("row")
    partial_w = lax.dot_general(
        kernel, random_cols, (((0,), (0,)), ((), ())), preferred_element_type=jnp.float32
    ).astype(jnp.bfloat16)
    pieces = lax.all_to_all(partial_w, "row", split_axis=0, concat_axis=0, tiled=True)
    piece = jnp.sum(pieces.reshape(parts, -1, width).astype(jnp.float32), axis=0)
    sample_w = lax.all_gather(piece.astype(jnp.bfloat16), "row", axis=0, tiled=True)
    return bases_of(reduce_panels(kernel, sample_w), tree_perm, leaf_units)


def reduce_panels(kernel, sample_w):
    columns = lax.axis_size("col")
    me = lax.axis_index("col")
    rows_dev = kernel.shape[0] // columns
    ring = columns // 2
    place, side = me // 2, me % 2
    swap = [(i, i ^ 1) for i in range(columns)]
    ahead = [(i, (i + 2) % columns) for i in range(columns)]
    owned = []
    for step in range(ring):
        target = lax.rem(place + ring - 1 - step, ring)
        panel = lax.dynamic_slice_in_dim(kernel, target * 2 * rows_dev, 2 * rows_dev)
        product = jnp.dot(panel, sample_w, preferred_element_type=jnp.float32)
        lower, upper = product[:rows_dev], product[rows_dev:]
        theirs = jnp.where(side == 0, upper, lower).astype(jnp.bfloat16)
        mine = jnp.where(side == 0, lower, upper)
        owned.append((mine, lax.ppermute(theirs, "col", swap)))
    total = None
    for mine, theirs in owned:
        here = mine + theirs.astype(jnp.float32)
        if total is not None:
            here = here + lax.ppermute(total, "col", ahead).astype(jnp.float32)
        total = here.astype(jnp.bfloat16)
    return total


def solution(mesh):
    return jax.shard_map(
        shards,
        mesh=mesh,
        in_specs=(P("row", "col"), P("row", None), P(), P()),
        out_specs=P(None, ("row", "col"), None),
        check_vma=False,
    )
```
